128 devices in a mesh: lev: 8 (over z, y_lo), mem: 16 (over x, y_hi, core).
Axes of the slice: x: 4, y: 4 (y_hi: 2, y_lo: 2; y = y_hi * 2 + y_lo), z: 4, core: 2. Of those that a mesh axis runs over, the one named last changes fastest.
Arguments:
- perturbations: bfloat16 [64, 2, 128, 256, 256], P('mem', None, 'lev'), may hold values from -6 to 6
- gradient: bfloat16 [2, 128, 256, 256], P(None, 'lev', 'mem'), may hold values from -6 to 6
- member_scale: int32 [64], P('mem'), may hold values from 0 to 3
- kernel_y: bfloat16 [4, 256, 256], replicated, may hold values from 0 to 1, as said below
- kernel_x: bfloat16 [4, 256, 256], replicated, may hold values from 0 to 1, as said below
- vertical_weights: float32 [4, 5], replicated, may hold values from 0.2 to 1
- layer_index: int32 [128], replicated, may hold values from 0 to 15, never falling along the last dimension, each value on 1 to 16 neighbouring positions
Outputs:
- increment: float32 [2, 128, 256, 256], P(None, 'lev', 'mem')
The draws below stay inside these ranges and needn't reach their ends.
Inputs may be any that keep to these rules, and one draw needn't show every extreme that they name: `layer_index`: layer numbers never fall from one level to the next; every layer has at least one level and at most 16. `kernel_y`: each scale's matrix has nonnegative entries and rows that sum to one. `kernel_x`: each scale's matrix has nonnegative entries and rows that sum to one.
All inputs are finite; a program needn't handle non-finite values.
Results may differ from the reference program's by a relative error of at most 0.0039.
Values may be sent and summed in bfloat16 or wider, within the bound.
No kernel may reach another device: no remote copies, remote signals or barrier semaphores. Data moves between devices by JAX's collectives and lax.ppermute only.
A program may use at most 128 MiB of HBM per device.

```python
import math
import jax
import jax.numpy as jnp
import numpy as np
from jax import lax

NY = 256
NX = 256
SCALES = 4
LEVELS = 128
MEMBERS = 64


def kernel_table(key, width):
    places = jnp.arange(width, dtype=jnp.float32)
    distance = jnp.abs(places[:, None] - places[None, :])
    length = 1.5 * 3.0 ** jnp.arange(SCALES, dtype=jnp.float32)
    rough = jax.random.uniform(key, (SCALES, width, width), jnp.float32, 0.5, 1.5)
    table = jnp.exp(-distance[None] / length[:, None, None]) * rough
    return (table / jnp.sum(table, axis=2, keepdims=True)).astype(jnp.bfloat16)


def draw_kernel_y(key, part):
    return kernel_table(jax.random.fold_in(key, 11), NY)


def draw_kernel_x(key, part):
    return kernel_table(jax.random.fold_in(key, 23), NX)


def touch_ends(result, own_key, least, largest):
    longest = result.shape.index(max(result.shape))
    spots = []
    for shift in (0, 1):
        where = [jax.random.randint(jax.random.fold_in(own_key, axis), (), 0, length) for axis, length in enumerate(result.shape)]
        where[longest] = (where[longest] + shift) % result.shape[longest]
        spots.append(tuple(where))
    return result.at[spots[0]].set(least).at[spots[1]].set(largest)


def spiked(entries, own_key, source, target, shards_of, factor):
    def block_of(axis_at):
        return (jnp.arange(entries.shape[axis_at]) // (entries.shape[axis_at] // shards_of)).reshape((-1,) + (1,) * (entries.ndim - 1 - axis_at))

    first = jax.random.permutation(own_key, shards_of)[block_of(target)]
    second = (block_of(target) + shards_of // 2) % shards_of
    return jnp.where((block_of(source) == first) | (block_of(source) == second), factor * entries, entries)


def block_scale(own_key, extent, split, low, largest):
    def one(axis_at, parts):
        draws = jax.random.uniform(jax.random.fold_in(jax.random.fold_in(own_key, 6), axis_at), (parts,), jnp.float32, low / len(split), largest / len(split))
        return jnp.repeat(jnp.exp(draws), extent[axis_at] // parts).reshape((-1,) + (1,) * (len(extent) - axis_at - 1))

    gain = one(*split[0])
    for cut in split[1:]:
        gain = gain * one(*cut)
    return gain


def profile(amount, total, bound, lean):
    loads = [(1 << 20) // math.isqrt(standing ** lean) + 1 for standing in range(2, amount + 1)]
    rest, counts = total - bound - (amount - 1), [1] * (amount - 1)
    while rest > 0:
        candidates = [i for i in range(amount - 1) if counts[i] < bound]
        mass, remaining = sum([loads[i] for i in candidates]), rest
        for i in candidates:
            more = min(bound - counts[i], max(1, remaining * loads[i] // mass), rest)
            counts[i] = counts[i] + more
            rest = rest - more
    return np.array([bound] + counts)


def ragged(key, count, total, most, lean):
    if count == 2:
        one = jax.random.randint(key, (), max(1, total - most), min(most, total - 1) + 1)
        return jnp.stack([one, total - one])
    tallies = jnp.asarray(profile(count, total, most, lean), jnp.int32)
    couples = (count - 1) // 2
    source_of, sink = tallies[1:1 + 2 * couples:2], tallies[2:2 + 2 * couples:2]
    slack = jnp.minimum(source_of - 1, most - sink)
    passed = jax.random.randint(jax.random.fold_in(key, 1), (couples,), 0, 1 << 20) % (slack + 1)
    tallies = tallies.at[1:1 + 2 * couples:2].set(source_of - passed).at[2:2 + 2 * couples:2].set(sink + passed)
    return tallies[jax.random.permutation(jax.random.fold_in(key, 2), count)]


def scatter_about(key, dims, scale, most, pieces=(), kind=jnp.bfloat16):
    result = scale * jax.random.normal(key, dims, jnp.float32)
    if pieces:
        result = result * block_scale(key, dims, pieces, -0.22, 0.18)
    return jnp.clip(result, -most, most).astype(kind)


def bell_draw_with(rng, extent, spread, reach, cuts, heavy, held_as=jnp.bfloat16):
    result = spread * jax.random.normal(rng, extent, jnp.float32)
    if cuts:
        result = result * block_scale(rng, extent, cuts, -0.22, 0.18)
    return jnp.clip(spiked(result, jax.random.fold_in(rng, 3), *heavy), -reach, reach).astype(held_as)


def setup_inputs(seed: int = 0) -> dict:
    key_list = jax.random.split(jax.random.key(seed), 8)
    return {
        "perturbations": bell_draw_with(key_list[0], (MEMBERS, 2, LEVELS, NY, NX), 1.0, 6.0, ((0, 16), (2, 8)), (0, 3, 16, 2.0)),
        "gradient": scatter_about(key_list[1], (2, LEVELS, NY, NX), 1.0, 6.0, ((1, 8), (2, 16))),
        "member_scale": touch_ends(jax.random.randint(key_list[2], (MEMBERS,), 0, SCALES), jax.random.fold_in(key_list[2], 1), 0, SCALES - 1).astype(jnp.int32),
        "kernel_y": draw_kernel_y(jax.random.fold_in(key_list[7], 71), 0),
        "kernel_x": draw_kernel_x(jax.random.fold_in(key_list[7], 71), 0),
        "vertical_weights": jnp.clip(jax.random.uniform(key_list[5], (SCALES, 5), jnp.float32, 0.2, 1.0), 0.2, 1.0),
        "layer_index": jnp.searchsorted(jnp.cumsum(ragged(key_list[6], max(3, LEVELS // 8), LEVELS, min(16, LEVELS // 2), 0)), jnp.arange(LEVELS), side="right").astype(jnp.int32),
    }


def reference(perturbations, gradient, member_scale, kernel_y, kernel_x, vertical_weights, layer_index):
    levels = perturbations.shape[2]
    grad_full = gradient.astype(jnp.float32)
    padded_ids = jnp.pad(layer_index, 2, constant_values=-1)

    def step(total, inputs):
        member, scale = inputs
        product = (member.astype(jnp.float32) * grad_full).astype(jnp.bfloat16)
        rows_k = jnp.einsum("ij,vljx->vlix", kernel_y[scale].astype(jnp.float32), product.astype(jnp.float32), precision=lax.Precision.HIGHEST).astype(jnp.bfloat16)
        horizontal = jnp.einsum("vlib,ab->vlia", rows_k.astype(jnp.float32), kernel_x[scale].astype(jnp.float32), precision=lax.Precision.HIGHEST).astype(jnp.bfloat16)
        padded = jnp.pad(horizontal.astype(jnp.float32), ((0, 0), (2, 2), (0, 0), (0, 0)))
        mixed = jnp.zeros(horizontal.shape, jnp.float32)
        for offset in range(-2, 3):
            same = (padded_ids[2 + offset:2 + offset + levels] == layer_index).astype(jnp.float32)
            mixed = mixed + vertical_weights[scale, offset + 2] * same[None, :, None, None] * padded[:, 2 + offset:2 + offset + levels]
        return total + member.astype(jnp.float32) * mixed, None

    total, _ = lax.scan(step, jnp.zeros(gradient.shape, jnp.float32), (perturbations, member_scale))
    return total / (perturbations.shape[0] - 1)
```

```python
import functools

import jax
import jax.numpy as jnp
from jax import lax
from jax.experimental import pallas as pl
from jax.experimental.pallas import tpu as pltpu
from jax.sharding import PartitionSpec as P


NXC, NH, NC = 4, 2, 2
BF = jnp.bfloat16
F32 = jnp.float32


def pairs_of(dx, dh, dc):
    out = []
    for x in range(NXC):
        for h in range(NH):
            for c in range(NC):
                dest = ((x + dx) % NXC) * 4 + ((h + dh) % NH) * 2 + (c + dc) % NC
                out.append((x * 4 + h * 2 + c, dest))
    return out


def move(value, dx=0, dh=0, dc=0):
    return lax.ppermute(value, "mem", pairs_of(dx, dh, dc))


def shift(value, pairs):
    return lax.ppermute(value, "lev", pairs)


def rows_at(mem, j, hr, cr):
    x = mem // 4
    h = (mem // 2) % 2
    c = mem % 2
    block = ((x + j) % 4) * 4 + ((h + hr) % 2) * 2 + (c + cr) % 2
    return pl.multiple_of(block * 16, 16)


def field(p, g, ky, kxt):
    product = p * g
    rows = jnp.dot(ky, product, preferred_element_type=F32).astype(BF)
    return jnp.dot(rows, kxt, preferred_element_type=F32).astype(BF)


def own_kernel(
    ms_ref, li_ref, ids_ref, w_ref, p_ref, q_ref, ky_ref, kxt_ref, *rest, levels, inv
):
    pieces = rest[:8]
    send_ref, keep_ref, hedge_ref, gs, acc, *rings = rest[8:]
    t = pl.program_id(0)
    mem = ids_ref[0]
    base = ids_ref[1] * levels

    @pl.when(t == 0)
    def _():
        for ring in rings:
            for slot in (3, 4):
                ring[slot] = jnp.zeros(ring.shape[1:], F32)

    lo = t - 2
    level = jnp.minimum(t, levels - 1)
    newest = lax.rem(t, 5)
    slots = [lax.rem(t + 1 + d, 5) for d in range(5)]

    def coef(k, d):
        other = lo + d
        a = jnp.clip(base + lo, 0, 127)
        b = jnp.clip(base + other, 0, 127)
        ok = (other >= 0) & (other < levels) & (li_ref[a] == li_ref[b])
        return jnp.where(ok, w_ref[ms_ref[k], d + 2], 0.0) * inv

    for cr in range(2):
        for hr in range(2):
            for j in range(4):
                block = pieces[cr * 4 + j][hr * levels + level]
                gs[pl.ds(rows_at(mem, j, hr, cr), 16), :] = block
    g = gs[...]

    for k in range(4):
        s = ms_ref[k]
        rings[k][newest] = field(p_ref[k, 0, 0], g, ky_ref[s], kxt_ref[s]).astype(F32)
        cs = [coef(k, d) for d in range(-2, 3)]
        for cr in range(2):
            for hr in range(2):
                for j in range(4):
                    place = cr * 8 + hr * 4 + j
                    r0 = rows_at(mem, j, hr, cr)
                    mix = None
                    for d in range(5):
                        term = cs[d] * rings[k][slots[d], pl.ds(r0, 16), :]
                        mix = term if mix is None else mix + term
                    mix = mix * q_ref[k, 0, 0, pl.ds(r0, 16), :].astype(F32)
                    if k:
                        mix = mix + acc[place]
                    if k < 3:
                        acc[place] = mix
                    elif cr:
                        send_ref[0, j, hr] = mix.astype(BF)
                    else:
                        keep_ref[0, j, hr] = mix

    @pl.when((t == 1) | (t == levels - 2))
    def _():
        for k in range(4):
            hedge_ref[0, k] = rings[k][newest].astype(BF)


def own_part(v, ms, li, ids, w, p, ky, kxt, pieces, inv):
    levels = p.shape[2]
    smem = pl.BlockSpec(memory_space=pltpu.SMEM)
    whole = pl.BlockSpec((4, 256, 256), lambda t, *_: (0, 0, 0))
    pblock = (4, 1, 1, 256, 256)
    part = pl.BlockSpec((1, 4, 2, 16, 256), lambda t, *_: (jnp.maximum(t - 2, 0), 0, 0, 0, 0))
    return pl.pallas_call(
        functools.partial(own_kernel, levels=levels, inv=inv),
        grid_spec=pltpu.PrefetchScalarGridSpec(
            num_scalar_prefetch=3,
            grid=(levels + 2,),
            in_specs=[
                smem,
                pl.BlockSpec(pblock, lambda t, *_: (0, v, jnp.minimum(t, levels - 1), 0, 0)),
                pl.BlockSpec(pblock, lambda t, *_: (0, v, jnp.maximum(t - 2, 0), 0, 0)),
                whole,
                whole,
            ]
            + [pl.BlockSpec((2 * levels, 16, 256), lambda t, *_: (0, 0, 0))] * 8,
            out_specs=[
                part,
                part,
                pl.BlockSpec(
                    (1, 4, 256, 256), lambda t, *_: (jnp.where(t < levels - 2, 0, 1), 0, 0, 0)
                ),
            ],
            scratch_shapes=[
                pltpu.VMEM((256, 256), BF),
                pltpu.VMEM((16, 16, 256), F32),
            ]
            + [pltpu.VMEM((5, 256, 256), F32)] * 4,
        ),
        out_shape=[
            jax.ShapeDtypeStruct((levels, 4, 2, 16, 256), BF),
            jax.ShapeDtypeStruct((levels, 4, 2, 16, 256), F32),
            jax.ShapeDtypeStruct((2, 4, 256, 256), BF),
        ],
    )(ms, li, ids, w, p, p, ky, kxt, *pieces)


def edge_kernel(
    ms_ref, li_ref, ids_ref, w_ref, above_ref, below_ref, first_ref, last_ref, ky_ref, kxt_ref,
    hedge_ref, *rest, v, levels, inv
):
    pieces = rest[:8]
    send_ref, keep_ref, gs, hs = rest[8:]
    mem = ids_ref[0]
    base = ids_ref[1] * levels
    for side in range(2):
        top = side == 0
        halo_ref = above_ref if top else below_ref
        p_ref = first_ref if top else last_ref
        for cr in range(2):
            for j in range(4):
                piece = pieces[cr * 4 + j]
                gs[side, pl.ds(rows_at(mem, j, 0, cr), 16), :] = piece[4 + side * 2 + v]
                gs[side, pl.ds(rows_at(mem, j, 1, cr), 16), :] = piece[side * 2 + v]
        g = gs[side]
        for k in range(4):
            s = ms_ref[k]
            hs[side, k] = field(halo_ref[k, 0], g, ky_ref[s], kxt_ref[s]).astype(F32)
    for side in range(2):
        top = side == 0
        halo_ref = above_ref if top else below_ref
        p_ref = first_ref if top else last_ref
        far = base - 1 if top else base + levels
        near = base if top else base + levels - 1
        after = base + 1 if top else base + levels - 2
        inside = (far >= 0) & (far < 128)
        far_id = li_ref[jnp.clip(far, 0, 127)]
        ok1 = inside & (far_id == li_ref[near])
        ok2 = inside & (far_id == li_ref[after])

        def pick(k, place, ok):
            return jnp.where(ok, w_ref[ms_ref[k], place], 0.0) * inv

        c_near = [pick(k, 1 if top else 3, ok1) for k in range(4)]
        c_next = [pick(k, 0 if top else 4, ok2) for k in range(4)]
        c_back = [pick(k, 4 if top else 0, ok2) for k in range(4)]
        i_near = 0 if top else 1
        for cr in range(2):
            for j in range(4):
                for hr in range(2):
                    rows = pl.ds(rows_at(mem, j, hr, cr), 16)
                    a, b, e = None, None, None
                    for k in range(4):
                        h = hs[side, k, rows, :]
                        a_k = c_near[k] * (h * p_ref[k, 0, i_near, rows, :].astype(F32))
                        b_k = c_next[k] * (h * p_ref[k, 0, 1 - i_near, rows, :].astype(F32))
                        e_k = c_back[k] * (
                            hedge_ref[side, k, rows, :].astype(F32)
                            * halo_ref[k, 0, rows, :].astype(F32)
                        )
                        a = a_k if a is None else a + a_k
                        b = b_k if b is None else b + b_k
                        e = e_k if e is None else e + e_k
                    places = (0, 1) if top else (3, 2)
                    for n, value in zip((*places, 4 + side), (a, b, e)):
                        if cr:
                            send_ref[n, j, hr] = value.astype(BF)
                        else:
                            keep_ref[n, j, hr] = value


def edge_part(v, ms, li, ids, w, above, below, p, ky, kxt, hedges, lasts, inv):
    levels = p.shape[2]
    smem = pl.BlockSpec(memory_space=pltpu.SMEM)
    whole = pl.BlockSpec((4, 256, 256), lambda t, *_: (0, 0, 0))
    halo = pl.BlockSpec((4, 1, 256, 256), lambda t, *_: (0, v, 0, 0))
    part = pl.BlockSpec((6, 4, 2, 16, 256), lambda t, *_: (0, 0, 0, 0, 0))
    return pl.pallas_call(
        functools.partial(edge_kernel, v=v, levels=levels, inv=inv),
        grid_spec=pltpu.PrefetchScalarGridSpec(
            num_scalar_prefetch=3,
            grid=(1,),
            in_specs=[
                smem,
                halo,
                halo,
                pl.BlockSpec((4, 1, 2, 256, 256), lambda t, *_: (0, v, 0, 0, 0)),
                pl.BlockSpec((4, 1, 2, 256, 256), lambda t, *_: (0, v, levels // 2 - 1, 0, 0)),
                whole,
                whole,
                pl.BlockSpec((2, 4, 256, 256), lambda t, *_: (0, 0, 0, 0)),
            ]
            + [pl.BlockSpec((8, 16, 256), lambda t, *_: (2 * levels // 8, 0, 0))] * 8,
            out_specs=[part, part],
            scratch_shapes=[
                pltpu.VMEM((2, 256, 256), BF),
                pltpu.VMEM((2, 4, 256, 256), F32),
            ],
        ),
        out_shape=[
            jax.ShapeDtypeStruct((6, 4, 2, 16, 256), BF),
            jax.ShapeDtypeStruct((6, 4, 2, 16, 256), F32),
        ],
    )(ms, li, ids, w, above, below, p, p, ky, kxt, hedges, *lasts)


def gather_x(payload):
    got = {j: move(payload, dx=-j) for j in (1, 3, 2)}
    return [payload, got[1], got[2], got[3]]


def gather_c(pieces):
    return pieces + [move(piece, dc=1) for piece in pieces]


def scatter_rows(total):
    got = [move(total[:, j].astype(BF), dx=j) for j in (1, 3, 2)]
    mine = total[:, 0]
    for piece in got:
        mine = mine + piece.astype(F32)
    return mine[:, 0] + move(mine[:, 1].astype(BF), dh=1).astype(F32)


def per_device(
    perturbations, gradient, member_scale, kernel_y, kernel_x, vertical_weights, layer_index
):
    levels = perturbations.shape[2]
    inv = 1.0 / (perturbations.shape[0] * lax.axis_size("mem") - 1)
    count = lax.axis_size("lev")
    up = [(i, i + 1) for i in range(count - 1)]
    down = [(i + 1, i) for i in range(count - 1)]
    ids = jnp.stack([lax.axis_index("mem"), lax.axis_index("lev")]).astype(jnp.int32)
    kxt = jnp.swapaxes(kernel_x, 1, 2)

    other = [move(gradient[v], dh=1) for v in range(2)]
    g_halo = jnp.concatenate(
        [shift(gradient[:, levels - 1], up), shift(gradient[:, 0], down)],
        axis=0,
    )
    x0 = gather_x(jnp.concatenate([gradient[0], other[0]]))
    other_halo = move(g_halo, dh=1)
    x1 = gather_x(jnp.concatenate([gradient[1], other[1], other_halo, g_halo]))
    pieces = [gather_c(x0), gather_c(x1)]
    above = shift(perturbations[:, :, levels - 1], up)
    below = shift(perturbations[:, :, 0], down)

    outs = []
    for v in range(2):
        send, keep, hedges = own_part(
            v, member_scale, layer_index, ids, vertical_weights, perturbations,
            kernel_y, kxt, pieces[v], inv,
        )
        own = keep + move(send, dc=1).astype(F32)
        send, keep = edge_part(
            v, member_scale, layer_index, ids, vertical_weights, above, below,
            perturbations, kernel_y, kxt, hedges, pieces[1], inv,
        )
        edge = keep + move(send, dc=1).astype(F32)
        total = jnp.concatenate(
            [
                own[:2] + edge[:2],
                own[2 : levels - 2],
                own[levels - 2 :] + edge[2:4],
                edge[4:],
            ]
        )
        mine = scatter_rows(total)
        from_above = shift(mine[levels + 1], up)
        from_below = shift(mine[levels], down)
        outs.append(
            jnp.concatenate(
                [
                    (mine[0] + from_above)[None],
                    mine[1 : levels - 1],
                    (mine[levels - 1] + from_below)[None],
                ]
            )
        )
    return jnp.stack(outs)


def solution(mesh):
    placed = (
        P("mem", None, "lev", None, None),
        P(None, "lev", "mem", None),
        P("mem"),
        P(),
        P(),
        P(),
        P(),
    )
    return jax.shard_map(
        per_device,
        mesh=mesh,
        in_specs=placed,
        out_specs=P(None, "lev", "mem", None),
        check_vma=False,
    )
```

```python
import functools

import jax
import jax.numpy as jnp
from jax import lax
from jax.experimental import pallas as pl
from jax.experimental.pallas import tpu as pltpu
from jax.sharding import PartitionSpec as P


NXC, NH, NC = 4, 2, 2
BF = jnp.bfloat16
F32 = jnp.float32


def pairs_of(dx, dh, dc):
    out = []
    for x in range(NXC):
        for h in range(NH):
            for c in range(NC):
                dest = ((x + dx) % NXC) * 4 + ((h + dh) % NH) * 2 + (c + dc) % NC
                out.append((x * 4 + h * 2 + c, dest))
    return out


def move(value, dx=0, dh=0, dc=0):
    return lax.ppermute(value, "mem", pairs_of(dx, dh, dc))


def shift(value, pairs):
    return lax.ppermute(value, "lev", pairs)


def rows_at(mem, j, hr, cr):
    x = mem // 4
    h = (mem // 2) % 2
    c = mem % 2
    block = ((x + j) % 4) * 4 + ((h + hr) % 2) * 2 + (c + cr) % 2
    return pl.multiple_of(block * 16, 16)


def field(p, g, ky, kx):
    product = p * g
    rows = jnp.dot(ky, product, preferred_element_type=F32).astype(BF)
    smoothed = lax.dot_general(
        rows, kx, (((1,), (1,)), ((), ())), preferred_element_type=F32
    )
    return smoothed.astype(BF)


def own_kernel(
    ms_ref, li_ref, ids_ref, w_ref, p_ref, q_ref, ky_ref, kx_ref, *rest, levels, inv
):
    pieces = rest[:8]
    send_ref, keep_ref, gs, acc, *rings = rest[8:]
    t = pl.program_id(0)
    mem = ids_ref[0]
    base = ids_ref[1] * levels

    @pl.when(t == 0)
    def _():
        for ring in rings:
            for slot in (3, 4):
                ring[slot] = jnp.zeros(ring.shape[1:], F32)

    lo = t - 2
    level = jnp.minimum(t, levels - 1)
    newest = lax.rem(t, 5)
    slots = [lax.rem(t + 1 + d, 5) for d in range(5)]

    def coef(k, d):
        other = lo + d
        a = jnp.clip(base + lo, 0, 127)
        b = jnp.clip(base + other, 0, 127)
        ok = (other >= 0) & (other < levels) & (li_ref[a] == li_ref[b])
        return jnp.where(ok, w_ref[ms_ref[k], d + 2], 0.0) * inv

    for cr in range(2):
        for hr in range(2):
            for j in range(4):
                block = pieces[cr * 4 + j][hr * levels + level]
                gs[pl.ds(rows_at(mem, j, hr, cr), 16), :] = block
    g = gs[...]

    for k in range(4):
        s = ms_ref[k]
        rings[k][newest] = field(p_ref[k, 0, 0], g, ky_ref[s], kx_ref[s]).astype(F32)
        cs = [coef(k, d) for d in range(-2, 3)]
        for cr in range(2):
            for hr in range(2):
                for j in range(4):
                    place = cr * 8 + hr * 4 + j
                    r0 = rows_at(mem, j, hr, cr)
                    mix = None
                    for d in range(5):
                        term = cs[d] * rings[k][slots[d], pl.ds(r0, 16), :]
                        mix = term if mix is None else mix + term
                    mix = mix * q_ref[k, 0, 0, pl.ds(r0, 16), :].astype(F32)
                    if k:
                        mix = mix + acc[place]
                    if k < 3:
                        acc[place] = mix
                    elif cr:
                        send_ref[j, hr, 0] = mix.astype(BF)
                    else:
                        keep_ref[j, hr, 0] = mix


def own_part(v, ms, li, ids, w, p, ky, kx, pieces, inv):
    levels = p.shape[2]
    smem = pl.BlockSpec(memory_space=pltpu.SMEM)
    whole = pl.BlockSpec((4, 256, 256), lambda t, *_: (0, 0, 0))
    pblock = (4, 1, 1, 256, 256)
    part = pl.BlockSpec((4, 2, 1, 16, 256), lambda t, *_: (0, 0, jnp.maximum(t - 2, 0), 0, 0))
    return pl.pallas_call(
        functools.partial(own_kernel, levels=levels, inv=inv),
        grid_spec=pltpu.PrefetchScalarGridSpec(
            num_scalar_prefetch=3,
            grid=(levels + 2,),
            in_specs=[
                smem,
                pl.BlockSpec(pblock, lambda t, *_: (0, v, jnp.minimum(t, levels - 1), 0, 0)),
                pl.BlockSpec(pblock, lambda t, *_: (0, v, jnp.maximum(t - 2, 0), 0, 0)),
                whole,
                whole,
            ]
            + [pl.BlockSpec((2 * levels, 16, 256), lambda t, *_: (0, 0, 0))] * 8,
            out_specs=[part, part],
            scratch_shapes=[
                pltpu.VMEM((256, 256), BF),
                pltpu.VMEM((16, 16, 256), F32),
            ]
            + [pltpu.VMEM((5, 256, 256), F32)] * 4,
        ),
        out_shape=[
            jax.ShapeDtypeStruct((4, 2, levels, 16, 256), BF),
            jax.ShapeDtypeStruct((4, 2, levels, 16, 256), F32),
        ],
    )(ms, li, ids, w, p, p, ky, kx, *pieces)


def edge_kernel(
    ms_ref, li_ref, ids_ref, w_ref, above_ref, below_ref, first_ref, last_ref, ky_ref, kx_ref,
    *rest, v, levels, inv
):
    pieces, lasts = rest[:8], rest[8:16]
    send_ref, keep_ref, gs, hs = rest[16:]
    mem = ids_ref[0]
    base = ids_ref[1] * levels
    for side in range(2):
        top = side == 0
        halo_ref = above_ref if top else below_ref
        p_ref = first_ref if top else last_ref
        level = 1 if top else levels - 2
        for cr in range(2):
            for j in range(4):
                last, piece = lasts[cr * 4 + j], pieces[cr * 4 + j]
                for hr in range(2):
                    rows = pl.ds(rows_at(mem, j, hr, cr), 16)
                    gs[2 * side, rows, :] = last[(4 - 4 * hr) + side * 2 + v]
                    gs[2 * side + 1, rows, :] = piece[hr * levels + level]
        for k in range(4):
            s = ms_ref[k]
            hs[2 * side, k] = field(halo_ref[k, 0], gs[2 * side], ky_ref[s], kx_ref[s])
            hs[2 * side + 1, k] = field(
                p_ref[k, 0, 1 if top else 0], gs[2 * side + 1], ky_ref[s], kx_ref[s]
            )
    for side in range(2):
        top = side == 0
        halo_ref = above_ref if top else below_ref
        p_ref = first_ref if top else last_ref
        far = base - 1 if top else base + levels
        near = base if top else base + levels - 1
        after = base + 1 if top else base + levels - 2
        inside = (far >= 0) & (far < 128)
        far_id = li_ref[jnp.clip(far, 0, 127)]
        ok1 = inside & (far_id == li_ref[near])
        ok2 = inside & (far_id == li_ref[after])

        def pick(k, place, ok):
            return jnp.where(ok, w_ref[ms_ref[k], place], 0.0) * inv

        c_near = [pick(k, 1 if top else 3, ok1) for k in range(4)]
        c_next = [pick(k, 0 if top else 4, ok2) for k in range(4)]
        c_back = [pick(k, 4 if top else 0, ok2) for k in range(4)]
        i_near = 0 if top else 1
        for cr in range(2):
            for j in range(4):
                for hr in range(2):
                    rows = pl.ds(rows_at(mem, j, hr, cr), 16)
                    a, b, e = None, None, None
                    for k in range(4):
                        h = hs[2 * side, k, rows, :].astype(F32)
                        a_k = c_near[k] * (h * p_ref[k, 0, i_near, rows, :].astype(F32))
                        b_k = c_next[k] * (h * p_ref[k, 0, 1 - i_near, rows, :].astype(F32))
                        e_k = c_back[k] * (
                            hs[2 * side + 1, k, rows, :].astype(F32)
                            * halo_ref[k, 0, rows, :].astype(F32)
                        )
                        a = a_k if a is None else a + a_k
                        b = b_k if b is None else b + b_k
                        e = e_k if e is None else e + e_k
                    places = (0, 1) if top else (3, 2)
                    for n, value in zip((*places, 4 + side), (a, b, e)):
                        if cr:
                            send_ref[j, hr, n] = value.astype(BF)
                        else:
                            keep_ref[j, hr, n] = value


def edge_part(v, ms, li, ids, w, above, below, p, ky, kx, pieces, lasts, inv):
    levels = p.shape[2]
    smem = pl.BlockSpec(memory_space=pltpu.SMEM)
    whole = pl.BlockSpec((4, 256, 256), lambda t, *_: (0, 0, 0))
    halo = pl.BlockSpec((4, 1, 256, 256), lambda t, *_: (0, v, 0, 0))
    part = pl.BlockSpec((4, 2, 6, 16, 256), lambda t, *_: (0, 0, 0, 0, 0))
    return pl.pallas_call(
        functools.partial(edge_kernel, v=v, levels=levels, inv=inv),
        grid_spec=pltpu.PrefetchScalarGridSpec(
            num_scalar_prefetch=3,
            grid=(1,),
            in_specs=[
                smem,
                halo,
                halo,
                pl.BlockSpec((4, 1, 2, 256, 256), lambda t, *_: (0, v, 0, 0, 0)),
                pl.BlockSpec((4, 1, 2, 256, 256), lambda t, *_: (0, v, levels // 2 - 1, 0, 0)),
                whole,
                whole,
            ]
            + [pl.BlockSpec((2 * levels, 16, 256), lambda t, *_: (0, 0, 0))] * 8
            + [pl.BlockSpec((8, 16, 256), lambda t, *_: (2 * levels // 8, 0, 0))] * 8,
            out_specs=[part, part],
            scratch_shapes=[
                pltpu.VMEM((4, 256, 256), BF),
                pltpu.VMEM((4, 4, 256, 256), BF),
            ],
        ),
        out_shape=[
            jax.ShapeDtypeStruct((4, 2, 6, 16, 256), BF),
            jax.ShapeDtypeStruct((4, 2, 6, 16, 256), F32),
        ],
    )(ms, li, ids, w, above, below, p, p, ky, kx, *pieces, *lasts)


def gather_x(payload):
    got = {j: move(payload, dx=-j) for j in (1, 3, 2)}
    return [payload, got[1], got[2], got[3]]


def gather_c(pieces):
    return pieces + [move(piece, dc=1) for piece in pieces]


def scatter_rows(total):
    got = [move(total[j].astype(BF), dx=j) for j in (1, 3, 2)]
    mine = total[0]
    for piece in got:
        mine = mine + piece.astype(F32)
    return mine[0] + move(mine[1].astype(BF), dh=1).astype(F32)


def per_device(
    perturbations, gradient, member_scale, kernel_y, kernel_x, vertical_weights, layer_index
):
    levels = perturbations.shape[2]
    inv = 1.0 / (perturbations.shape[0] * lax.axis_size("mem") - 1)
    count = lax.axis_size("lev")
    up = [(i, i + 1) for i in range(count - 1)]
    down = [(i + 1, i) for i in range(count - 1)]
    ids = jnp.stack([lax.axis_index("mem"), lax.axis_index("lev")]).astype(jnp.int32)

    gh_up = shift(gradient[:, levels - 1], up)
    gh_down = shift(gradient[:, 0], down)
    other = move(gradient[0], dh=1)
    later = jnp.concatenate([gradient[1], gh_up, gh_down])
    other_later = move(later, dh=1)
    p_last, p_first = perturbations[:, :, levels - 1], perturbations[:, :, 0]
    above = shift(p_last, up)
    below = shift(p_first, down)
    x0 = gather_x(jnp.concatenate([gradient[0], other]))
    x1 = gather_x(jnp.concatenate([later[:levels], other_later, later[levels:]]))
    pieces = [gather_c(x0), gather_c(x1)]

    def own_sums(v):
        send, keep = own_part(
            v, member_scale, layer_index, ids, vertical_weights, perturbations,
            kernel_y, kernel_x, pieces[v], inv,
        )
        return keep + move(send, dc=1).astype(F32)

    def edge_sums(v):
        send, keep = edge_part(
            v, member_scale, layer_index, ids, vertical_weights, above, below,
            perturbations, kernel_y, kernel_x, pieces[v], pieces[1], inv,
        )
        return keep + move(send, dc=1).astype(F32)

    def joined(own, edge):
        return [
            own[:, :, :2] + edge[:, :, :2],
            own[:, :, 2 : levels - 2],
            own[:, :, levels - 2 :] + edge[:, :, 2:4],
        ]

    def closed(mine, from_above, from_below):
        return jnp.concatenate(
            [
                (mine[0] + from_above)[None],
                mine[1 : levels - 1],
                (mine[levels - 1] + from_below)[None],
            ]
        )

    own = own_sums(0)
    edges = [edge_sums(0), edge_sums(1)]
    later = lax.optimization_barrier(edges[1][:, :, :4])
    total = jnp.concatenate(
        joined(own, edges[0]) + [edges[0][:, :, 4:], edges[1][:, :, 4:]], axis=2
    )
    first = scatter_rows(total)
    backs = first[levels:].reshape((2, 2) + first.shape[1:])
    from_above = shift(backs[:, 1], up)
    from_below = shift(backs[:, 0], down)
    second = scatter_rows(jnp.concatenate(joined(own_sums(1), later), axis=2))
    return jnp.stack(
        [
            closed(first[:levels], from_above[0], from_below[0]),
            closed(second, from_above[1], from_below[1]),
        ]
    )


def solution(mesh):
    placed = (
        P("mem", None, "lev", None, None),
        P(None, "lev", "mem", None),
        P("mem"),
        P(),
        P(),
        P(),
        P(),
    )
    return jax.shard_map(
        per_device,
        mesh=mesh,
        in_specs=placed,
        out_specs=P(None, "lev", "mem", None),
        check_vma=False,
    )
```

```python
import functools

import jax
import jax.numpy as jnp
from jax import lax
from jax.experimental import pallas as pl
from jax.experimental.pallas import tpu as pltpu
from jax.sharding import PartitionSpec as P


NXC, NH, NC = 4, 2, 2
BF = jnp.bfloat16
F32 = jnp.float32


def pairs_of(dx, dh, dc):
    out = []
    for x in range(NXC):
        for h in range(NH):
            for c in range(NC):
                dest = ((x + dx) % NXC) * 4 + ((h + dh) % NH) * 2 + (c + dc) % NC
                out.append((x * 4 + h * 2 + c, dest))
    return out


def move(value, dx=0, dh=0, dc=0):
    return lax.ppermute(value, "mem", pairs_of(dx, dh, dc))


def shift(value, pairs):
    return lax.ppermute(value, "lev", pairs)


def rows_at(mem, j, hr, cr):
    x = mem // 4
    h = (mem // 2) % 2
    c = mem % 2
    block = ((x + j) % 4) * 4 + ((h + hr) % 2) * 2 + (c + cr) % 2
    return pl.multiple_of(block * 16, 16)


def field(p, g, ky, kx):
    product = p * g
    rows = jnp.dot(ky, product, preferred_element_type=F32).astype(BF)
    smoothed = lax.dot_general(
        rows, kx, (((1,), (1,)), ((), ())), preferred_element_type=F32
    )
    return smoothed.astype(BF)


def own_kernel(
    ms_ref, li_ref, ids_ref, w_ref, p_ref, q_ref, ky_ref, kx_ref, *rest, levels, inv
):
    pieces = rest[:8]
    send_ref, keep_ref, gs, acc, fresh, *rings = rest[8:]
    u = pl.program_id(0)
    mem = ids_ref[0]
    base = ids_ref[1] * levels

    @pl.when(u == 0)
    def _():
        for ring in rings:
            ring[4] = jnp.zeros(ring.shape[1:], F32)
            ring[5] = jnp.zeros(ring.shape[1:], F32)
        fresh[...] = jnp.zeros(fresh.shape, F32)

    pair = 2 * jnp.minimum(u, levels // 2 - 1)
    slots = [lax.rem(2 * u + d, 6) for d in range(6)]

    def coef(k, lo, d):
        other = lo + d
        a = jnp.clip(base + lo, 0, 127)
        b = jnp.clip(base + other, 0, 127)
        ok = (other >= 0) & (other < levels) & (li_ref[a] == li_ref[b])
        return jnp.where(ok, w_ref[ms_ref[k], d + 2], 0.0) * inv

    for i in range(2):
        for cr in range(2):
            for hr in range(2):
                for j in range(4):
                    block = pieces[cr * 4 + j][hr * levels + pair + i]
                    gs[i, pl.ds(rows_at(mem, j, hr, cr), 16), :] = block

    for k in range(4):
        for i in range(2):
            rings[k][slots[4 + i]] = fresh[i, k]

    gate = None
    for i in range(2):
        g = gs[i]
        for k in range(4):
            s = ms_ref[k]
            rows = jnp.dot(ky_ref[s], p_ref[k, 0, i] * g, preferred_element_type=F32)
            gate = rows if gate is None else gate
            fresh[i, k] = lax.dot_general(
                rows.astype(BF), kx_ref[s], (((1,), (1,)), ((), ())), preferred_element_type=F32
            )

    for i in range(2):
        for k in range(4):
            if i == 0:
                rings[k][6, 0:8, 0:128] = gate[0:8, 0:128]
            cs = [coef(k, 2 * u - 4 + i, d) for d in range(-2, 3)]
            for cr in range(2):
                for hr in range(2):
                    for j in range(4):
                        place = cr * 8 + hr * 4 + j
                        r0 = rows_at(mem, j, hr, cr)
                        mix = None
                        for d in range(5):
                            term = cs[d] * rings[k][slots[i + d], pl.ds(r0, 16), :]
                            mix = term if mix is None else mix + term
                        mix = mix * q_ref[k, 0, i, pl.ds(r0, 16), :].astype(F32)
                        if k:
                            mix = mix + acc[i, place]
                        if k < 3:
                            acc[i, place] = mix
                        elif cr:
                            send_ref[j, hr, i] = mix.astype(BF)
                        else:
                            keep_ref[j, hr, i] = mix


def own_part(v, ms, li, ids, w, p, ky, kx, pieces, inv):
    levels = p.shape[2]
    smem = pl.BlockSpec(memory_space=pltpu.SMEM)
    whole = pl.BlockSpec((4, 256, 256), lambda u, *_: (0, 0, 0))
    pblock = (4, 1, 2, 256, 256)
    part = pl.BlockSpec((4, 2, 2, 16, 256), lambda u, *_: (0, 0, jnp.maximum(u - 2, 0), 0, 0))
    return pl.pallas_call(
        functools.partial(own_kernel, levels=levels, inv=inv),
        grid_spec=pltpu.PrefetchScalarGridSpec(
            num_scalar_prefetch=3,
            grid=(levels // 2 + 2,),
            in_specs=[
                smem,
                pl.BlockSpec(
                    pblock, lambda u, *_: (0, v, jnp.minimum(u, levels // 2 - 1), 0, 0)
                ),
                pl.BlockSpec(pblock, lambda u, *_: (0, v, jnp.maximum(u - 2, 0), 0, 0)),
                whole,
                whole,
            ]
            + [pl.BlockSpec((2 * levels, 16, 256), lambda u, *_: (0, 0, 0))] * 8,
            out_specs=[part, part],
            scratch_shapes=[
                pltpu.VMEM((2, 256, 256), BF),
                pltpu.VMEM((2, 16, 16, 256), F32),
                pltpu.VMEM((2, 4, 256, 256), F32),
            ]
            + [pltpu.VMEM((7, 256, 256), F32)] * 4,
        ),
        out_shape=[
            jax.ShapeDtypeStruct((4, 2, levels, 16, 256), BF),
            jax.ShapeDtypeStruct((4, 2, levels, 16, 256), F32),
        ],
    )(ms, li, ids, w, p, p, ky, kx, *pieces)


def edge_kernel(
    ms_ref, li_ref, ids_ref, w_ref, above_ref, below_ref, first_ref, last_ref, ky_ref, kx_ref,
    *rest, v, levels, inv
):
    pieces, lasts = rest[:8], rest[8:16]
    send_ref, keep_ref, gs, hs = rest[16:]
    mem = ids_ref[0]
    base = ids_ref[1] * levels
    for side in range(2):
        top = side == 0
        halo_ref = above_ref if top else below_ref
        p_ref = first_ref if top else last_ref
        level = 1 if top else levels - 2
        for cr in range(2):
            for j in range(4):
                last, piece = lasts[cr * 4 + j], pieces[cr * 4 + j]
                for hr in range(2):
                    rows = pl.ds(rows_at(mem, j, hr, cr), 16)
                    gs[2 * side, rows, :] = last[(4 - 4 * hr) + side * 2 + v]
                    gs[2 * side + 1, rows, :] = piece[hr * levels + level]
        for k in range(4):
            s = ms_ref[k]
            hs[2 * side, k] = field(halo_ref[k, 0], gs[2 * side], ky_ref[s], kx_ref[s])
            hs[2 * side + 1, k] = field(
                p_ref[k, 0, 1 if top else 0], gs[2 * side + 1], ky_ref[s], kx_ref[s]
            )
    for side in range(2):
        top = side == 0
        halo_ref = above_ref if top else below_ref
        p_ref = first_ref if top else last_ref
        far = base - 1 if top else base + levels
        near = base if top else base + levels - 1
        after = base + 1 if top else base + levels - 2
        inside = (far >= 0) & (far < 128)
        far_id = li_ref[jnp.clip(far, 0, 127)]
        ok1 = inside & (far_id == li_ref[near])
        ok2 = inside & (far_id == li_ref[after])

        def pick(k, place, ok):
            return jnp.where(ok, w_ref[ms_ref[k], place], 0.0) * inv

        c_near = [pick(k, 1 if top else 3, ok1) for k in range(4)]
        c_next = [pick(k, 0 if top else 4, ok2) for k in range(4)]
        c_back = [pick(k, 4 if top else 0, ok2) for k in range(4)]
        i_near = 0 if top else 1
        for cr in range(2):
            for j in range(4):
                for hr in range(2):
                    rows = pl.ds(rows_at(mem, j, hr, cr), 16)
                    a, b, e = None, None, None
                    for k in range(4):
                        h = hs[2 * side, k, rows, :].astype(F32)
                        a_k = c_near[k] * (h * p_ref[k, 0, i_near, rows, :].astype(F32))
                        b_k = c_next[k] * (h * p_ref[k, 0, 1 - i_near, rows, :].astype(F32))
                        e_k = c_back[k] * (
                            hs[2 * side + 1, k, rows, :].astype(F32)
                            * halo_ref[k, 0, rows, :].astype(F32)
                        )
                        a = a_k if a is None else a + a_k
                        b = b_k if b is None else b + b_k
                        e = e_k if e is None else e + e_k
                    places = (0, 1) if top else (3, 2)
                    for n, value in zip((*places, 4 + side), (a, b, e)):
                        if cr:
                            send_ref[j, hr, n] = value.astype(BF)
                        else:
                            keep_ref[j, hr, n] = value


def edge_part(v, ms, li, ids, w, above, below, p, ky, kx, pieces, lasts, inv):
    levels = p.shape[2]
    smem = pl.BlockSpec(memory_space=pltpu.SMEM)
    whole = pl.BlockSpec((4, 256, 256), lambda t, *_: (0, 0, 0))
    halo = pl.BlockSpec((4, 1, 256, 256), lambda t, *_: (0, v, 0, 0))
    part = pl.BlockSpec((4, 2, 6, 16, 256), lambda t, *_: (0, 0, 0, 0, 0))
    return pl.pallas_call(
        functools.partial(edge_kernel, v=v, levels=levels, inv=inv),
        grid_spec=pltpu.PrefetchScalarGridSpec(
            num_scalar_prefetch=3,
            grid=(1,),
            in_specs=[
                smem,
                halo,
                halo,
                pl.BlockSpec((4, 1, 2, 256, 256), lambda t, *_: (0, v, 0, 0, 0)),
                pl.BlockSpec((4, 1, 2, 256, 256), lambda t, *_: (0, v, levels // 2 - 1, 0, 0)),
                whole,
                whole,
            ]
            + [pl.BlockSpec((2 * levels, 16, 256), lambda t, *_: (0, 0, 0))] * 8
            + [pl.BlockSpec((8, 16, 256), lambda t, *_: (2 * levels // 8, 0, 0))] * 8,
            out_specs=[part, part],
            scratch_shapes=[
                pltpu.VMEM((4, 256, 256), BF),
                pltpu.VMEM((4, 4, 256, 256), BF),
            ],
        ),
        out_shape=[
            jax.ShapeDtypeStruct((4, 2, 6, 16, 256), BF),
            jax.ShapeDtypeStruct((4, 2, 6, 16, 256), F32),
        ],
    )(ms, li, ids, w, above, below, p, p, ky, kx, *pieces, *lasts)


def gather_x(payload):
    got = {j: move(payload, dx=-j) for j in (1, 3, 2)}
    return [payload, got[1], got[2], got[3]]


def gather_c(pieces):
    return pieces + [move(piece, dc=1) for piece in pieces]


def scatter_rows(total):
    got = [move(total[j].astype(BF), dx=j) for j in (1, 3, 2)]
    mine = total[0]
    for piece in got:
        mine = mine + piece.astype(F32)
    return mine[0] + move(mine[1].astype(BF), dh=1).astype(F32)


def per_device(
    perturbations, gradient, member_scale, kernel_y, kernel_x, vertical_weights, layer_index
):
    levels = perturbations.shape[2]
    inv = 1.0 / (perturbations.shape[0] * lax.axis_size("mem") - 1)
    count = lax.axis_size("lev")
    up = [(i, i + 1) for i in range(count - 1)]
    down = [(i + 1, i) for i in range(count - 1)]
    ids = jnp.stack([lax.axis_index("mem"), lax.axis_index("lev")]).astype(jnp.int32)

    gh_up = shift(gradient[:, levels - 1], up)
    gh_down = shift(gradient[:, 0], down)
    other = move(gradient[0], dh=1)
    later = jnp.concatenate([gradient[1], gh_up, gh_down])
    other_later = move(later, dh=1)
    p_last, p_first = perturbations[:, :, levels - 1], perturbations[:, :, 0]
    above = shift(p_last, up)
    below = shift(p_first, down)
    x0 = gather_x(jnp.concatenate([gradient[0], other]))
    x1 = gather_x(jnp.concatenate([later[:levels], other_later, later[levels:]]))
    pieces = [gather_c(x0), gather_c(x1)]

    def own_sums(v):
        send, keep = own_part(
            v, member_scale, layer_index, ids, vertical_weights, perturbations,
            kernel_y, kernel_x, pieces[v], inv,
        )
        return keep + move(send, dc=1).astype(F32)

    def edge_sums(v):
        send, keep = edge_part(
            v, member_scale, layer_index, ids, vertical_weights, above, below,
            perturbations, kernel_y, kernel_x, pieces[v], pieces[1], inv,
        )
        return keep + move(send, dc=1).astype(F32)

    def joined(own, edge):
        return [
            own[:, :, :2] + edge[:, :, :2],
            own[:, :, 2 : levels - 2],
            own[:, :, levels - 2 :] + edge[:, :, 2:4],
        ]

    def closed(mine, from_above, from_below):
        return jnp.concatenate(
            [
                (mine[0] + from_above)[None],
                mine[1 : levels - 1],
                (mine[levels - 1] + from_below)[None],
            ]
        )

    own = own_sums(0)
    edges = [edge_sums(0), edge_sums(1)]
    later = lax.optimization_barrier(edges[1][:, :, :4])
    total = jnp.concatenate(
        joined(own, edges[0]) + [edges[0][:, :, 4:], edges[1][:, :, 4:]], axis=2
    )
    first = scatter_rows(total)
    backs = first[levels:].reshape((2, 2) + first.shape[1:])
    from_above = shift(backs[:, 1], up)
    from_below = shift(backs[:, 0], down)
    second = scatter_rows(jnp.concatenate(joined(own_sums(1), later), axis=2))
    return jnp.stack(
        [
            closed(first[:levels], from_above[0], from_below[0]),
            closed(second, from_above[1], from_below[1]),
        ]
    )


def solution(mesh):
    placed = (
        P("mem", None, "lev", None, None),
        P(None, "lev", "mem", None),
        P("mem"),
        P(),
        P(),
        P(),
        P(),
    )
    return jax.shard_map(
        per_device,
        mesh=mesh,
        in_specs=placed,
        out_specs=P(None, "lev", "mem", None),
        check_vma=False,
    )
```

```python
import functools

import jax
import jax.numpy as jnp
from jax import lax
from jax.experimental import pallas as pl
from jax.experimental.pallas import tpu as pltpu
from jax.sharding import PartitionSpec as P


NXC, NH, NC = 4, 2, 2
BF = jnp.bfloat16
F32 = jnp.float32


def pairs_of(dx, dh, dc):
    out = []
    for x in range(NXC):
        for h in range(NH):
            for c in range(NC):
                dest = ((x + dx) % NXC) * 4 + ((h + dh) % NH) * 2 + (c + dc) % NC
                out.append((x * 4 + h * 2 + c, dest))
    return out


def move(value, dx=0, dh=0, dc=0):
    return lax.ppermute(value, "mem", pairs_of(dx, dh, dc))


def shift(value, pairs):
    return lax.ppermute(value, "lev", pairs)


def rows_at(mem, j, hr, cr):
    x = mem // 4
    h = (mem // 2) % 2
    c = mem % 2
    block = ((x + j) % 4) * 4 + ((h + hr) % 2) * 2 + (c + cr) % 2
    return pl.multiple_of(block * 16, 16)


def field(p, g, ky, kx):
    product = p * g
    rows = jnp.dot(ky, product, preferred_element_type=F32).astype(BF)
    smoothed = lax.dot_general(
        rows, kx, (((1,), (1,)), ((), ())), preferred_element_type=F32
    )
    return smoothed.astype(BF)


def own_kernel(
    ms_ref, li_ref, ids_ref, w_ref, p_ref, q_ref, ky_ref, kx_ref, *rest, levels, inv
):
    pieces = rest[:8]
    send_ref, keep_ref, gs, acc, fresh, *rings = rest[8:]
    u = pl.program_id(0)
    mem = ids_ref[0]
    base = ids_ref[1] * levels

    @pl.when(u == 0)
    def _():
        for ring in rings:
            ring[4] = jnp.zeros(ring.shape[1:], F32)
            ring[5] = jnp.zeros(ring.shape[1:], F32)
        fresh[...] = jnp.zeros(fresh.shape, F32)

    pair = 2 * jnp.minimum(u, levels // 2 - 1)
    slots = [lax.rem(2 * u + d, 6) for d in range(6)]

    def coef(k, lo, d):
        other = lo + d
        a = jnp.clip(base + lo, 0, 127)
        b = jnp.clip(base + other, 0, 127)
        ok = (other >= 0) & (other < levels) & (li_ref[a] == li_ref[b])
        return jnp.where(ok, w_ref[ms_ref[k], d + 2], 0.0) * inv

    for i in range(2):
        for cr in range(2):
            for hr in range(2):
                for j in range(4):
                    block = pieces[cr * 4 + j][hr * levels + pair + i]
                    gs[i, pl.ds(rows_at(mem, j, hr, cr), 16), :] = block

    for k in range(4):
        for i in range(2):
            rings[k][slots[4 + i]] = fresh[i, k]

    gate = None
    for i in range(2):
        g = gs[i]
        for k in range(4):
            s = ms_ref[k]
            rows = jnp.dot(ky_ref[s], p_ref[k, 0, i] * g, preferred_element_type=F32)
            gate = rows if gate is None else gate
            fresh[i, k] = lax.dot_general(
                rows.astype(BF), kx_ref[s], (((1,), (1,)), ((), ())), preferred_element_type=F32
            )

    for i in range(2):
        for k in range(4):
            if i == 0:
                rings[k][6, 0:8, 0:128] = gate[0:8, 0:128]
            cs = [coef(k, 2 * u - 4 + i, d) for d in range(-2, 3)]
            for cr in range(2):
                for hr in range(2):
                    for j in range(4):
                        place = cr * 8 + hr * 4 + j
                        r0 = rows_at(mem, j, hr, cr)
                        mix = None
                        for d in range(5):
                            term = cs[d] * rings[k][slots[i + d], pl.ds(r0, 16), :]
                            mix = term if mix is None else mix + term
                        mix = mix * q_ref[k, 0, i, pl.ds(r0, 16), :].astype(F32)
                        if k:
                            mix = mix + acc[i, place]
                        if k < 3:
                            acc[i, place] = mix
                        elif cr:
                            send_ref[j, hr, i] = mix.astype(BF)
                        else:
                            keep_ref[j, hr, i] = mix


def own_part(v, ms, li, ids, w, p, ky, kx, pieces, inv):
    levels = p.shape[2]
    smem = pl.BlockSpec(memory_space=pltpu.SMEM)
    whole = pl.BlockSpec((4, 256, 256), lambda u, *_: (0, 0, 0))
    pblock = (4, 1, 2, 256, 256)
    part = pl.BlockSpec((4, 2, 2, 16, 256), lambda u, *_: (0, 0, jnp.maximum(u - 2, 0), 0, 0))
    return pl.pallas_call(
        functools.partial(own_kernel, levels=levels, inv=inv),
        grid_spec=pltpu.PrefetchScalarGridSpec(
            num_scalar_prefetch=3,
            grid=(levels // 2 + 2,),
            in_specs=[
                smem,
                pl.BlockSpec(
                    pblock, lambda u, *_: (0, v, jnp.minimum(u, levels // 2 - 1), 0, 0)
                ),
                pl.BlockSpec(pblock, lambda u, *_: (0, v, jnp.maximum(u - 2, 0), 0, 0)),
                whole,
                whole,
            ]
            + [pl.BlockSpec((2 * levels, 16, 256), lambda u, *_: (0, 0, 0))] * 8,
            out_specs=[part, part],
            scratch_shapes=[
                pltpu.VMEM((2, 256, 256), BF),
                pltpu.VMEM((2, 16, 16, 256), F32),
                pltpu.VMEM((2, 4, 256, 256), F32),
            ]
            + [pltpu.VMEM((7, 256, 256), F32)] * 4,
        ),
        out_shape=[
            jax.ShapeDtypeStruct((4, 2, levels, 16, 256), BF),
            jax.ShapeDtypeStruct((4, 2, levels, 16, 256), F32),
        ],
    )(ms, li, ids, w, p, p, ky, kx, *pieces)


def edge_kernel(
    ms_ref, li_ref, ids_ref, w_ref, above_ref, below_ref, first_ref, last_ref, ky_ref, kx_ref,
    *rest, levels, inv
):
    pieces, lasts = rest[:64], rest[64:72]
    send_ref, keep_ref, gs, hs = rest[72:]
    v = pl.program_id(0)
    mem = ids_ref[0]
    base = ids_ref[1] * levels
    for cr in range(2):
        for j in range(4):
            for hr in range(2):
                rows = pl.ds(rows_at(mem, j, hr, cr), 16)
                for side in range(2):
                    place = ((4 - 4 * hr) + side * 2) + v
                    gs[2 * side, rows, :] = lasts[cr * 4 + j][place]
    for var in range(2):

        @pl.when(v == var)
        def _():
            for cr in range(2):
                for j in range(4):
                    for hr in range(2):
                        rows = pl.ds(rows_at(mem, j, hr, cr), 16)
                        for side in range(2):
                            n = ((var * 8 + cr * 4 + j) * 2 + hr) * 2 + side
                            gs[2 * side + 1, rows, :] = pieces[n][0]

    for side in range(2):
        top = side == 0
        halo_ref = above_ref if top else below_ref
        p_ref = first_ref if top else last_ref
        for k in range(4):
            s = ms_ref[k]
            hs[2 * side, k] = field(halo_ref[k, 0], gs[2 * side], ky_ref[s], kx_ref[s])
            hs[2 * side + 1, k] = field(
                p_ref[k, 0, 1 if top else 0], gs[2 * side + 1], ky_ref[s], kx_ref[s]
            )
    for side in range(2):
        top = side == 0
        halo_ref = above_ref if top else below_ref
        p_ref = first_ref if top else last_ref
        far = base - 1 if top else base + levels
        near = base if top else base + levels - 1
        after = base + 1 if top else base + levels - 2
        inside = (far >= 0) & (far < 128)
        far_id = li_ref[jnp.clip(far, 0, 127)]
        ok1 = inside & (far_id == li_ref[near])
        ok2 = inside & (far_id == li_ref[after])

        def pick(k, place, ok):
            return jnp.where(ok, w_ref[ms_ref[k], place], 0.0) * inv

        c_near = [pick(k, 1 if top else 3, ok1) for k in range(4)]
        c_next = [pick(k, 0 if top else 4, ok2) for k in range(4)]
        c_back = [pick(k, 4 if top else 0, ok2) for k in range(4)]
        i_near = 0 if top else 1
        for cr in range(2):
            for j in range(4):
                for hr in range(2):
                    rows = pl.ds(rows_at(mem, j, hr, cr), 16)
                    a, b, e = None, None, None
                    for k in range(4):
                        h = hs[2 * side, k, rows, :].astype(F32)
                        a_k = c_near[k] * (h * p_ref[k, 0, i_near, rows, :].astype(F32))
                        b_k = c_next[k] * (h * p_ref[k, 0, 1 - i_near, rows, :].astype(F32))
                        e_k = c_back[k] * (
                            hs[2 * side + 1, k, rows, :].astype(F32)
                            * halo_ref[k, 0, rows, :].astype(F32)
                        )
                        a = a_k if a is None else a + a_k
                        b = b_k if b is None else b + b_k
                        e = e_k if e is None else e + e_k
                    places = (0, 1) if top else (3, 2)
                    for n, value in zip((*places, 4 + side), (a, b, e)):
                        if cr:
                            send_ref[0, j, hr, n] = value.astype(BF)
                        else:
                            keep_ref[0, j, hr, n] = value


def edge_part(ms, li, ids, w, above, below, p, ky, kx, pieces, inv):
    levels = p.shape[2]
    smem = pl.BlockSpec(memory_space=pltpu.SMEM)
    whole = pl.BlockSpec((4, 256, 256), lambda v, *_: (0, 0, 0))
    halo = pl.BlockSpec((4, 1, 256, 256), lambda v, *_: (0, v, 0, 0))
    part = pl.BlockSpec((1, 4, 2, 6, 16, 256), lambda v, *_: (v, 0, 0, 0, 0, 0))
    specs, operands = [], []
    for var in range(2):
        for piece in pieces[var]:
            for hr in range(2):
                for level in (1, levels - 2):
                    place = hr * levels + level
                    specs.append(
                        pl.BlockSpec((1, 16, 256), lambda v, *_, place=place: (place, 0, 0))
                    )
                    operands.append(piece)
    return pl.pallas_call(
        functools.partial(edge_kernel, levels=levels, inv=inv),
        grid_spec=pltpu.PrefetchScalarGridSpec(
            num_scalar_prefetch=3,
            grid=(2,),
            in_specs=[
                smem,
                halo,
                halo,
                pl.BlockSpec((4, 1, 2, 256, 256), lambda v, *_: (0, v, 0, 0, 0)),
                pl.BlockSpec((4, 1, 2, 256, 256), lambda v, *_: (0, v, levels // 2 - 1, 0, 0)),
                whole,
                whole,
            ]
            + specs
            + [pl.BlockSpec((8, 16, 256), lambda v, *_: (2 * levels // 8, 0, 0))] * 8,
            out_specs=[part, part],
            scratch_shapes=[
                pltpu.VMEM((4, 256, 256), BF),
                pltpu.VMEM((4, 4, 256, 256), BF),
            ],
        ),
        out_shape=[
            jax.ShapeDtypeStruct((2, 4, 2, 6, 16, 256), BF),
            jax.ShapeDtypeStruct((2, 4, 2, 6, 16, 256), F32),
        ],
        name="edge",
    )(ms, li, ids, w, above, below, p, p, ky, kx, *operands, *pieces[1])


def gather_x(payload):
    got = {j: move(payload, dx=-j) for j in (1, 3, 2)}
    return [payload, got[1], got[2], got[3]]


def gather_c(pieces):
    return pieces + [move(piece, dc=1) for piece in pieces]


def scatter_x(parts):
    return [move(part, dx=j) for j, part in zip((1, 3, 2), parts)]


def scatter_h(total, got):
    mine = total[0]
    for piece in got:
        mine = mine + piece.astype(F32)
    return mine[0] + move(mine[1].astype(BF), dh=1).astype(F32)


def shares(total):
    return [total[j].astype(BF) for j in (1, 3, 2)]


def per_device(
    perturbations, gradient, member_scale, kernel_y, kernel_x, vertical_weights, layer_index
):
    levels = perturbations.shape[2]
    inv = 1.0 / (perturbations.shape[0] * lax.axis_size("mem") - 1)
    count = lax.axis_size("lev")
    up = [(i, i + 1) for i in range(count - 1)]
    down = [(i + 1, i) for i in range(count - 1)]
    ids = jnp.stack([lax.axis_index("mem"), lax.axis_index("lev")]).astype(jnp.int32)

    gh_up = shift(gradient[:, levels - 1], up)
    gh_down = shift(gradient[:, 0], down)
    other = move(gradient[0], dh=1)
    later = jnp.concatenate([gradient[1], gh_up, gh_down])
    other_later = move(later, dh=1)
    p_last, p_first = perturbations[:, :, levels - 1], perturbations[:, :, 0]
    above = shift(p_last, up)
    below = shift(p_first, down)
    x0 = gather_x(jnp.concatenate([gradient[0], other]))
    x1 = gather_x(jnp.concatenate([later[:levels], other_later, later[levels:]]))
    pieces = [gather_c(x0), gather_c(x1)]

    def own_sums(v):
        send, keep = own_part(
            v, member_scale, layer_index, ids, vertical_weights, perturbations,
            kernel_y, kernel_x, pieces[v], inv,
        )
        return keep + move(send, dc=1).astype(F32)

    def edge_sums():
        send, keep = edge_part(
            member_scale, layer_index, ids, vertical_weights, above, below,
            perturbations, kernel_y, kernel_x, pieces, inv,
        )
        received = move(send, dc=1)
        return [keep[v] + received[v].astype(F32) for v in range(2)]

    def joined(own, edge):
        return [
            own[:, :, :2] + edge[:, :, :2],
            own[:, :, 2 : levels - 2],
            own[:, :, levels - 2 :] + edge[:, :, 2:4],
        ]

    def closed(mine, from_above, from_below):
        return jnp.concatenate(
            [
                (mine[0] + from_above)[None],
                mine[1 : levels - 1],
                (mine[levels - 1] + from_below)[None],
            ]
        )

    own = own_sums(0)
    edges = edge_sums()
    later = lax.optimization_barrier(edges[1][:, :, :4])
    total = jnp.concatenate(
        joined(own, edges[0]) + [edges[0][:, :, 4:], edges[1][:, :, 4:]], axis=2
    )
    got = scatter_x(shares(total))
    total1 = jnp.concatenate(joined(own_sums(1), later), axis=2)
    parts = shares(total1)
    second = scatter_h(total1, scatter_x(parts))
    first = scatter_h(total, got)
    backs = first[levels:].reshape((2, 2) + first.shape[1:])
    from_above = shift(backs[:, 1], up)
    from_below = shift(backs[:, 0], down)
    return jnp.stack(
        [
            closed(first[:levels], from_above[0], from_below[0]),
            closed(second, from_above[1], from_below[1]),
        ]
    )


def solution(mesh):
    placed = (
        P("mem", None, "lev", None, None),
        P(None, "lev", "mem", None),
        P("mem"),
        P(),
        P(),
        P(),
        P(),
    )
    return jax.shard_map(
        per_device,
        mesh=mesh,
        in_specs=placed,
        out_specs=P(None, "lev", "mem", None),
        check_vma=False,
    )
```
